256 devices in a mesh: cube: 8 (over x, y_lo), blk: 32 (over z, y_hi, core).
Axes of the slice: x: 4, y: 4 (y_hi: 2, y_lo: 2; y = y_hi * 2 + y_lo), z: 8, core: 2. Of those that a mesh axis runs over, the one named last changes fastest.
Arguments:
- updates: float32 [8, 32, 8, 128, 128], P('cube', 'blk'), may hold values from -6 to 6
- pivot_panel: float32 [16384, 256], P(('cube', 'blk')), may hold values from -1.5 to 1.5
- map_low: int32 [8, 32, 8], P('cube', 'blk'), may hold values from 0 to 7
- map_own: int32 [8, 32, 8], P('cube', 'blk'), may hold values from 0 to 63
- map_out: int32 [8, 32, 8], P('cube', 'blk'), may hold values from 0 to 63
Outputs:
- schur: float32 [8, 32, 64, 16384], P(None, 'blk', None, 'cube')
The draws below stay inside these ranges and needn't reach their ends.
All inputs are finite; a program needn't handle non-finite values.
Results may differ from the reference program's by a relative error of at most 0.000058.
Values sent between devices are 32-bit elements; how exact they have to be, the bound alone decides.
A program may use at most 64 MiB of HBM per device.

```python
import jax
import jax.numpy as jnp
import numpy as np
from jax import lax

PR = 64
UB = 8
BS = 128
PANEL = 256
M = 16384
TB = 64
N_CUBE = 8
N_BLK = 32


def touch_ends(values, stream_key, low, high):
    shape = values.shape
    place = [jax.random.randint(jax.random.fold_in(stream_key, axis), (), 0, shape[axis]) for axis in range(len(shape))]
    values = values.at[tuple(place)].set(low)
    longest = shape.index(max(shape))
    place[longest] = (place[longest] + 1) % shape[longest]
    return values.at[tuple(place)].set(high)


def steps_of(own_key, extent, shards, smallest, high):
    gain = 1.0
    for axis_at, shards_of in shards:
        steps = jax.random.uniform(jax.random.fold_in(jax.random.fold_in(own_key, 6), axis_at), (shards_of,), jnp.float32, smallest / len(shards), high / len(shards))
        gain = gain * jnp.repeat(jnp.exp(steps), extent[axis_at] // shards_of).reshape((-1,) + (1,) * (len(extent) - 1 - axis_at))
    return gain


def normal_values(own_key, shape, scale, bound, shards=(), kind=jnp.bfloat16):
    entries = jax.random.normal(own_key, shape, jnp.float32) * scale
    if len(shards) > 0:
        entries = steps_of(own_key, shape, shards, -0.22, 0.18) * entries
    return jnp.clip(entries, min=-bound, max=bound).astype(kind)


def setup_inputs(seed: int = 0) -> dict:
    streams_of = jax.random.split(jax.random.key(seed), 6)
    updates = normal_values(streams_of[0], (N_CUBE, N_BLK, UB, BS, BS), 1.0, 6.0, ((0, 8), (1, 32)), jnp.float32)
    pivot_panel = normal_values(streams_of[1], (M, PANEL), 0.25, 1.5, ((0, 256),), jnp.float32)
    map_low = touch_ends(jax.random.randint(streams_of[2], (N_CUBE, N_BLK, UB), 0, UB), jax.random.fold_in(streams_of[2], 1), 0, UB - 1).astype(jnp.int32)
    map_own = touch_ends(jax.random.randint(streams_of[3], (N_CUBE, N_BLK, UB), 0, TB), jax.random.fold_in(streams_of[3], 1), 0, TB - 1).astype(jnp.int32)
    map_out = touch_ends(jax.random.randint(streams_of[4], (N_CUBE, N_BLK, UB), 0, TB), jax.random.fold_in(streams_of[4], 1), 0, TB - 1).astype(jnp.int32)
    return {"updates": updates, "pivot_panel": pivot_panel, "map_low": map_low, "map_own": map_own, "map_out": map_out}


exact_mode = lax.Precision.HIGHEST


def one_hot(targets, classes):
    return (targets[..., None] == jnp.arange(classes, dtype=jnp.int32)).astype(jnp.float32)


def reference(updates, pivot_panel, map_low, map_own, map_out):
    bit_count = N_CUBE.bit_length() - 1
    cube_ids = np.arange(N_CUBE)
    low_peer = cube_ids ^ (1 << (bit_count - 2))
    top_peer = cube_ids ^ (1 << (bit_count - 1))
    blocks = updates.reshape(N_CUBE, N_BLK, UB, BS * BS)
    outgoing = jnp.einsum("cbus,cbuk->cbsk", one_hot(map_low, UB), blocks, precision=exact_mode)
    merged = blocks + outgoing[low_peer]
    own_part = jnp.einsum("cbst,cbsk->cbtk", one_hot(map_own, TB), merged, precision=exact_mode)
    peer_part = jnp.einsum("cbst,cbsk->cbtk", one_hot(map_out, TB), merged, precision=exact_mode)
    tile_sums = own_part + peer_part[top_peer]
    row_count = N_CUBE * PR
    col_count = N_BLK * PR
    tile_grid = tile_sums.reshape(N_CUBE, N_BLK, row_count // BS, col_count // BS, BS, BS)
    tile_grid = tile_grid.transpose(0, 1, 2, 4, 3, 5).reshape(N_CUBE, N_BLK, N_CUBE, PR, col_count)
    front_block = tile_grid.transpose(2, 1, 3, 0, 4).reshape(N_CUBE, N_BLK, PR, N_CUBE * col_count)
    row_panel = pivot_panel.reshape(N_CUBE, N_BLK, PR, PANEL)
    product = jnp.einsum("abkp,jp->abkj", row_panel, pivot_panel, precision=exact_mode)
    return front_block - product
```

```python
import functools

import jax
import jax.numpy as jnp
from jax import lax
from jax.experimental import pallas as pl
from jax.experimental.pallas import tpu as pltpu
from jax.sharding import PartitionSpec as P

MESH = pl.DeviceIdType.MESH
CHUNKS = 16
PIECES = 2


def flip(index, bit):
    return index + bit - 2 * bit * lax.rem(lax.div(index, bit), 2)


def exchange_kernel(
    updates,
    panel,
    map_low,
    map_own,
    map_out,
    own_u,
    peer_u,
    upper_u,
    product,
    places,
    rows,
    cols,
    left,
    outgoing,
    relay_u,
    relay_map,
    low_scalars,
    local_sem,
    row_send,
    row_recv,
    col_send,
    col_recv,
    pair_send,
    pair_recv,
    upd_send,
    upd_recv,
    map_send,
    map_recv,
):
    cube, blk = lax.axis_index("cube"), lax.axis_index("blk")
    z_count = lax.axis_size("blk") // 4
    blk_count = 4 * z_count
    slots, tile = own_u.shape[0], own_u.shape[1]
    part = panel.shape[0]

    low = {"cube": flip(cube, 2), "blk": blk}
    across = {"cube": flip(flip(cube, 2), 4), "blk": blk}
    y_pair = {"cube": flip(cube, 1), "blk": blk}
    y_other = {"cube": flip(cube, 1), "blk": flip(blk, 2)}
    z_up = {"cube": cube, "blk": lax.rem(blk + 4, blk_count)}
    z_down = {"cube": cube, "blk": lax.rem(blk + blk_count - 4, blk_count)}
    pair = {"cube": cube, "blk": flip(blk, 1)}

    in_flight = []

    def send(src, dst, sems, at, device):
        copy = pltpu.make_async_remote_copy(
            src_ref=src,
            dst_ref=dst,
            send_sem=sems[0].at[at],
            recv_sem=sems[1].at[at],
            device_id=device,
            device_id_type=MESH,
        )
        copy.start()
        in_flight.append(copy)

    def arrived(dst, sems, at):
        pltpu.make_async_remote_copy(
            src_ref=dst,
            dst_ref=dst,
            send_sem=sems[0].at[at],
            recv_sem=sems[1].at[at],
            device_id=low,
            device_id_type=MESH,
        ).wait_recv()

    row_sems, col_sems = (row_send, row_recv), (col_send, col_recv)
    pair_sems, upd_sems = (pair_send, pair_recv), (upd_send, upd_recv)
    map_sems = (map_send, map_recv)

    def span(piece):
        return pl.ds(piece * (part // PIECES), part // PIECES)

    barrier = pltpu.get_barrier_semaphore()
    everyone = (low, across, y_pair, y_other, z_up, z_down, pair)
    for device in everyone:
        pl.semaphore_signal(barrier, inc=1, device_id=device, device_id_type=MESH)

    here = [
        pltpu.make_async_copy(map_low.at[0, 0], low_scalars, local_sem.at[0]),
        pltpu.make_async_copy(updates.at[0, 0], own_u, local_sem.at[1]),
        pltpu.make_async_copy(panel, rows.at[cube], local_sem.at[2]),
        pltpu.make_async_copy(panel, cols.at[blk], local_sem.at[3]),
        pltpu.make_async_copy(map_own.at[0, 0], places.at[0], local_sem.at[4]),
    ]
    for copy in here:
        copy.start()
    pl.semaphore_wait(barrier, len(everyone))

    def row_at(message, piece):
        return message * PIECES + piece

    def chunk_rows(chunk):
        return pl.ds(chunk * (tile // CHUNKS), tile // CHUNKS)

    for piece in range(PIECES):
        mine = panel.at[span(piece)]
        there = rows.at[cube, span(piece)]
        send(mine, there, row_sems, row_at(0, piece), low)
        send(mine, there, row_sems, row_at(1, piece), across)
        send(mine, there, row_sems, row_at(2, piece), y_pair)

    half = z_count // 2
    per_direction = (half - 1) * PIECES + 1

    def z_at(kind, direction, distance, piece):
        step = (distance - 1) * PIECES + (piece if distance < half else 0)
        return 2 + (kind * 2 + direction) * per_direction + step

    def z_slot(kind, direction, distance):
        shift = 4 * distance
        base = blk if kind == 0 else flip(blk, 2)
        return lax.rem(base + (blk_count - shift if direction == 0 else shift), blk_count)

    z_devices = (z_up, z_down)
    for piece in range(PIECES):
        for direction in range(2):
            send(
                panel.at[span(piece)],
                cols.at[blk, span(piece)],
                col_sems,
                z_at(0, direction, 1, piece),
                z_devices[direction],
            )
    send(panel, cols.at[blk], pair_sems, 0, pair)
    send(map_low.at[0, 0], places.at[1], map_sems, 0, low)
    send(map_out.at[0, 0], relay_map.at[0, 0], map_sems, 1, low)
    for chunk in range(CHUNKS):
        send(
            updates.at[0, 0, :, chunk_rows(chunk)],
            peer_u.at[:, chunk_rows(chunk)],
            upd_sems,
            chunk,
            low,
        )

    here[0].wait()
    here[1].wait()
    targets = [low_scalars[slot] for slot in range(slots)]

    @pl.loop(0, tile // 8)
    def _(step):
        at = pl.ds(pl.multiple_of(step * 8, 8), 8)
        blocks = [own_u[slot, at] for slot in range(slots)]
        for target in range(slots):
            terms = [
                blocks[slot] * jnp.where(targets[slot] == target, 1.0, 0.0)
                for slot in range(slots)
            ]
            while len(terms) > 1:
                terms = [a + b for a, b in zip(terms[::2], terms[1::2])]
            outgoing[target, at] = terms[0]

    low_slot = flip(cube, 2)
    across_slot = flip(flip(cube, 2), 4)
    upper_slot = flip(cube, 4)
    y_slot = flip(cube, 1)

    def row_event(message, slot, piece, forwards):
        there = rows.at[slot, span(piece)]
        arrived(there, row_sems, row_at(message, piece))
        for next_message, device in forwards:
            send(there, there, row_sems, row_at(next_message, piece), device)

    def y_relay(piece):
        there = rows.at[y_slot, span(piece)]
        arrived(there, row_sems, row_at(2, piece))
        send(there, cols.at[blk, span(piece)], col_sems, piece, y_other)

    def y_far(piece):
        there = cols.at[flip(blk, 2), span(piece)]
        arrived(there, col_sems, piece)
        for direction in range(2):
            send(there, there, col_sems, z_at(1, direction, 1, piece), z_devices[direction])
        if piece == PIECES - 1:
            whole = cols.at[flip(blk, 2)]
            send(whole, whole, pair_sems, 1, pair)

    def pair_at(kind, direction, distance):
        return 2 + (kind * 2 + direction) * half + distance - 1

    def z_event(kind, direction, distance, piece):
        slot = z_slot(kind, direction, distance)
        there = cols.at[slot, span(piece)]
        arrived(there, col_sems, z_at(kind, direction, distance, piece))
        last = distance == half
        onward = distance + 1 < half or (distance + 1 == half and piece == direction)
        if onward:
            at = z_at(kind, direction, distance + 1, piece)
            send(there, there, col_sems, at, z_devices[direction])
        if last:
            send(there, there, pair_sems, pair_at(kind, direction, distance), pair)
        elif piece == PIECES - 1:
            whole = cols.at[slot]
            send(whole, whole, pair_sems, pair_at(kind, direction, distance), pair)

    def chunk_event(chunk):
        at = chunk_rows(chunk)
        arrived(peer_u.at[:, at], upd_sems, chunk)
        relay_u[:, at] = peer_u[:, at] + outgoing[:, at]
        if chunk == 0:
            arrived(relay_map.at[0, 0], map_sems, 1)
            send(relay_map.at[0, 0], places.at[2], map_sems, 2, across)
        send(relay_u.at[:, at], upper_u.at[:, at], upd_sems, CHUNKS + chunk, across)

    piece_time, hop_time = 0.7, 1.65
    events = []

    def when(time, event, *operands):
        events.append((time, len(events), functools.partial(event, *operands)))

    hop = hop_time + piece_time
    for piece in range(PIECES):
        late = piece * piece_time
        when(hop + late, y_relay, piece)
        when(hop + late, row_event, 0, low_slot, piece, ((3, across), (4, y_pair)))
        when(hop + late, row_event, 1, across_slot, piece, ((5, y_pair),))
        when(2 * hop + late, y_far, piece)
        when(2 * hop + late, row_event, 3, upper_slot, piece, ((6, y_pair),))
        for kind in range(2):
            for distance in range(1, half + 1):
                for direction in range(2):
                    if distance < half or piece == direction:
                        time = hop * (distance + 2 * kind) + late
                        when(time, z_event, kind, direction, distance, piece)
    for chunk in range(CHUNKS):
        when(hop + piece_time * (chunk + PIECES), chunk_event, chunk)
    for _, _, event in sorted(events, key=lambda entry: entry[:2]):
        event()

    for message, bit in ((4, 2), (5, 6), (6, 4)):
        slot = flip(y_slot, 2) if bit != 4 else flip(y_slot, 4)
        slot = flip(slot, 4) if bit == 6 else slot
        for piece in range(PIECES):
            arrived(rows.at[slot, span(piece)], row_sems, row_at(message, piece))
    here[2].wait()
    here[3].wait()
    here[4].wait()

    depth = panel.shape[1]
    row_count = rows.shape[0] * part
    values = -rows[...].reshape(row_count, depth)
    high = values.astype(jnp.bfloat16)
    rest = (values - high.astype(jnp.float32)).astype(jnp.bfloat16)
    left[:, 0:depth] = high
    left[:, depth : 2 * depth] = high
    left[:, 2 * depth : 3 * depth] = rest

    def other(slot):
        return flip(slot, 1)

    arrived(cols.at[other(blk)], pair_sems, 0)
    arrived(cols.at[other(flip(blk, 2))], pair_sems, 1)
    for kind in range(2):
        for distance in range(1, half):
            for direction in range(2):
                slot = other(z_slot(kind, direction, distance))
                arrived(cols.at[slot], pair_sems, pair_at(kind, direction, distance))

    here_z = lax.div(blk, 4)
    group = 4 * part

    def multiply(z):
        right = cols[pl.ds(z * 4, 4)].reshape(group, depth)
        high = right.astype(jnp.bfloat16)
        rest = (right - high.astype(jnp.float32)).astype(jnp.bfloat16)
        right = jnp.concatenate([high, rest, high], axis=1)
        at = pl.ds(pl.multiple_of(z * group, group), group)
        product[:, at] = lax.dot_general(
            left[...],
            right,
            (((1,), (1,)), ((), ())),
            preferred_element_type=jnp.float32,
        )

    @pl.loop(0, z_count - 1)
    def _(step):
        multiply(lax.rem(here_z + half + 1 + step, z_count))

    for kind in range(2):
        for direction in range(2):
            slot = other(z_slot(kind, direction, half))
            at = pair_at(kind, direction, half)
            arrived(cols.at[slot, span(direction)], pair_sems, at)
    multiply(lax.rem(here_z + half, z_count))

    arrived(places.at[1], map_sems, 0)
    arrived(places.at[2], map_sems, 2)
    for chunk in range(CHUNKS):
        arrived(upper_u.at[:, chunk_rows(chunk)], upd_sems, CHUNKS + chunk)
    for copy in in_flight:
        copy.wait_send()


def place_kernel(
    product, own_u, peer_u, upper_u, places, out, front, sems
):
    slots, tile = own_u.shape[0], own_u.shape[1]
    tile_rows, tile_cols = front.shape[0] // tile, front.shape[1] // tile
    copies = []
    for tile_row in range(tile_rows):
        rows = pl.ds(tile_row * tile, tile)
        front[rows] = product[rows]

        def add(target, source, slot):
            @pl.when(lax.div(target, tile_cols) == tile_row)
            def _():
                col = lax.rem(target, tile_cols) * tile
                at = pl.ds(pl.multiple_of(col, tile), tile)
                front[rows, at] += source[slot]

        @pl.loop(0, slots)
        def _(slot):
            add(places[0, slot], own_u, slot)
            add(places[0, places[1, slot]], peer_u, slot)
            add(places[2, slot], upper_u, slot)

        copy = pltpu.make_async_copy(front.at[rows], out.at[rows], sems.at[tile_row])
        copy.start()
        copies.append(copy)
    for copy in copies:
        copy.wait()


def in_hbm(array):
    return pltpu.with_memory_space_constraint(array, pltpu.HBM)


def local(updates, pivot_panel, map_low, map_own, map_out):
    slots, tile = updates.shape[2], updates.shape[3]
    part, depth = pivot_panel.shape
    cubes, blks = lax.axis_size("cube"), lax.axis_size("blk")
    row_count, col_count = cubes * part, blks * part
    z_count = blks // 4
    half = z_count // 2
    f32, i32, bf16 = jnp.float32, jnp.int32, jnp.bfloat16
    dma = pltpu.SemaphoreType.DMA
    hbm = pl.BlockSpec(memory_space=pltpu.HBM)
    vmem = pl.BlockSpec(memory_space=pltpu.VMEM)
    smem = pl.BlockSpec(memory_space=pltpu.SMEM)
    z_messages = 2 + 4 * ((half - 1) * PIECES + 1)
    pair_messages = 2 + 4 * half
    blocks = pltpu.VMEM((slots, tile, tile), f32)
    own_u, peer_u, upper_u, product, places = pl.pallas_call(
        exchange_kernel,
        out_shape=(
            blocks,
            blocks,
            blocks,
            pltpu.VMEM((row_count, col_count), f32),
            pltpu.VMEM((3, slots), i32),
        ),
        in_specs=[hbm] * 5,
        out_specs=(vmem,) * 5,
        scratch_shapes=[
            pltpu.VMEM((cubes, part, depth), f32),
            pltpu.VMEM((blks, part, depth), f32),
            pltpu.VMEM((row_count, 3 * depth), bf16),
            pltpu.VMEM((slots, tile, tile), f32),
            pltpu.VMEM((slots, tile, tile), f32),
            pltpu.VMEM((1, 1, slots), i32),
            pltpu.SMEM((slots,), i32),
            dma((5,)),
            dma((7 * PIECES,)),
            dma((7 * PIECES,)),
            dma((z_messages,)),
            dma((z_messages,)),
            dma((pair_messages,)),
            dma((pair_messages,)),
            dma((2 * CHUNKS,)),
            dma((2 * CHUNKS,)),
            dma((3,)),
            dma((3,)),
        ],
        compiler_params=pltpu.CompilerParams(
            collective_id=0, has_side_effects=True, vmem_limit_bytes=24 << 20
        ),
    )(*(in_hbm(array) for array in (updates, pivot_panel, map_low, map_own, map_out)))
    out = pl.pallas_call(
        place_kernel,
        out_shape=jax.ShapeDtypeStruct((row_count, col_count), f32),
        in_specs=[vmem] * 4 + [smem],
        out_specs=hbm,
        scratch_shapes=[pltpu.VMEM((row_count, col_count), f32), dma((row_count // tile,))],
        compiler_params=pltpu.CompilerParams(vmem_limit_bytes=16 << 20),
    )(product, own_u, peer_u, upper_u, places)
    return out.reshape(cubes, 1, part, col_count)


def solution(mesh):
    placed = (
        P("cube", "blk", None, None, None),
        P(("cube", "blk"), None),
        P("cube", "blk", None),
        P("cube", "blk", None),
        P("cube", "blk", None),
    )
    return jax.shard_map(
        local, mesh=mesh, in_specs=placed, out_specs=P(None, "blk", None, "cube"), check_vma=False
    )
```

```python
import functools

import jax
import jax.numpy as jnp
from jax import lax
from jax.experimental import pallas as pl
from jax.experimental.pallas import tpu as pltpu
from jax.sharding import PartitionSpec as P

MESH = pl.DeviceIdType.MESH
CHUNKS = 16
PIECES = 2
FAR = 3
X_STEP = 0.55
Z_SHIFT = 0.0
Z_STEP = 2.3


def flip(index, bit):
    return index + bit - 2 * bit * lax.rem(lax.div(index, bit), 2)


def exchange_kernel(
    updates,
    panel,
    map_low,
    map_own,
    map_out,
    own_u,
    peer_u,
    upper_u,
    product,
    places,
    rows,
    cols,
    left,
    outgoing,
    relay_u,
    relay_map,
    low_scalars,
    local_sem,
    row_send,
    row_recv,
    col_send,
    col_recv,
    pair_send,
    pair_recv,
    upd_send,
    upd_recv,
    map_send,
    map_recv,
):
    cube, blk = lax.axis_index("cube"), lax.axis_index("blk")
    z_count = lax.axis_size("blk") // 4
    blk_count = 4 * z_count
    slots, tile = own_u.shape[0], own_u.shape[1]
    part = panel.shape[0]

    low = {"cube": flip(cube, 2), "blk": blk}
    across = {"cube": flip(flip(cube, 2), 4), "blk": blk}
    y_pair = {"cube": flip(cube, 1), "blk": blk}
    y_far = {"cube": cube, "blk": flip(blk, 2)}
    z_up = {"cube": cube, "blk": lax.rem(blk + 4, blk_count)}
    z_down = {"cube": cube, "blk": lax.rem(blk + blk_count - 4, blk_count)}
    pair = {"cube": cube, "blk": flip(blk, 1)}

    in_flight = []

    def send(src, dst, sems, at, device):
        copy = pltpu.make_async_remote_copy(
            src_ref=src,
            dst_ref=dst,
            send_sem=sems[0].at[at],
            recv_sem=sems[1].at[at],
            device_id=device,
            device_id_type=MESH,
        )
        copy.start()
        in_flight.append(copy)

    def arrived(dst, sems, at):
        pltpu.make_async_remote_copy(
            src_ref=dst,
            dst_ref=dst,
            send_sem=sems[0].at[at],
            recv_sem=sems[1].at[at],
            device_id=low,
            device_id_type=MESH,
        ).wait_recv()

    row_sems, col_sems = (row_send, row_recv), (col_send, col_recv)
    pair_sems, upd_sems = (pair_send, pair_recv), (upd_send, upd_recv)
    map_sems = (map_send, map_recv)

    def span(piece):
        return pl.ds(piece * (part // PIECES), part // PIECES)

    barrier = pltpu.get_barrier_semaphore()
    everyone = (low, across, y_pair, y_far, z_up, z_down, pair)
    for device in everyone:
        pl.semaphore_signal(barrier, inc=1, device_id=device, device_id_type=MESH)

    here = [
        pltpu.make_async_copy(map_low.at[0, 0], low_scalars, local_sem.at[0]),
        pltpu.make_async_copy(updates.at[0, 0], own_u, local_sem.at[1]),
        pltpu.make_async_copy(panel, rows.at[cube], local_sem.at[2]),
        pltpu.make_async_copy(panel, cols.at[blk], local_sem.at[3]),
        pltpu.make_async_copy(map_own.at[0, 0], places.at[0], local_sem.at[4]),
    ]
    for copy in here:
        copy.start()
    pl.semaphore_wait(barrier, len(everyone))

    def row_at(message, piece):
        return message * PIECES + piece

    def chunk_rows(chunk):
        return pl.ds(chunk * (tile // CHUNKS), tile // CHUNKS)

    for piece in range(PIECES):
        mine = panel.at[span(piece)]
        there = rows.at[cube, span(piece)]
        send(mine, there, row_sems, row_at(0, piece), low)
        send(mine, there, row_sems, row_at(1, piece), across)
        send(mine, there, row_sems, row_at(2, piece), y_pair)

    half = z_count // 2
    per_direction = (half - 1) * PIECES + 1

    def z_at(kind, direction, distance, piece):
        step = (distance - 1) * PIECES + (piece if distance < half else 0)
        return 2 + (kind * 2 + direction) * per_direction + step

    def z_slot(kind, direction, distance):
        shift = 4 * distance
        base = blk if kind == 0 else flip(blk, 2)
        return lax.rem(base + (blk_count - shift if direction == 0 else shift), blk_count)

    z_devices = (z_up, z_down)
    for piece in range(PIECES):
        for direction in range(2):
            send(
                panel.at[span(piece)],
                cols.at[blk, span(piece)],
                col_sems,
                z_at(0, direction, 1, piece),
                z_devices[direction],
            )
    for piece in range(PIECES):
        send(panel.at[span(piece)], cols.at[blk, span(piece)], col_sems, piece, y_far)
    send(panel, cols.at[blk], pair_sems, 0, pair)
    send(map_low.at[0, 0], places.at[1], map_sems, 0, low)
    send(map_out.at[0, 0], relay_map.at[0, 0], map_sems, 1, low)
    for chunk in range(CHUNKS):
        send(
            updates.at[0, 0, :, chunk_rows(chunk)],
            peer_u.at[:, chunk_rows(chunk)],
            upd_sems,
            chunk,
            low,
        )

    here[0].wait()
    here[1].wait()
    targets = [low_scalars[slot] for slot in range(slots)]

    @pl.loop(0, tile // 8)
    def _(step):
        at = pl.ds(pl.multiple_of(step * 8, 8), 8)
        blocks = [own_u[slot, at] for slot in range(slots)]
        for target in range(slots):
            terms = [
                blocks[slot] * jnp.where(targets[slot] == target, 1.0, 0.0)
                for slot in range(slots)
            ]
            while len(terms) > 1:
                terms = [a + b for a, b in zip(terms[::2], terms[1::2])]
            outgoing[target, at] = terms[0]

    low_slot = flip(cube, 2)
    across_slot = flip(flip(cube, 2), 4)
    upper_slot = flip(cube, 4)
    y_slot = flip(cube, 1)

    def row_event(message, slot, piece, forwards):
        there = rows.at[slot, span(piece)]
        arrived(there, row_sems, row_at(message, piece))
        for next_message, device in forwards:
            send(there, there, row_sems, row_at(next_message, piece), device)

    def far_event(piece):
        there = cols.at[flip(blk, 2), span(piece)]
        arrived(there, col_sems, piece)
        for direction in range(2):
            send(there, there, col_sems, z_at(1, direction, 1, piece), z_devices[direction])
        if piece == PIECES - 1:
            whole = cols.at[flip(blk, 2)]
            send(whole, whole, pair_sems, 1, pair)

    def pair_at(kind, direction, distance):
        return 2 + (kind * 2 + direction) * half + distance - 1

    def z_event(kind, direction, distance, piece):
        slot = z_slot(kind, direction, distance)
        there = cols.at[slot, span(piece)]
        arrived(there, col_sems, z_at(kind, direction, distance, piece))
        last = distance == half
        onward = distance + 1 < half or (distance + 1 == half and piece == direction)
        if kind == 1 and distance + 1 >= FAR:
            onward = False
        if kind == 0 and distance >= FAR:
            send(there, there, col_sems, z_at(1, direction, distance, piece), y_far)
        if onward:
            at = z_at(kind, direction, distance + 1, piece)
            send(there, there, col_sems, at, z_devices[direction])
        if last:
            send(there, there, pair_sems, pair_at(kind, direction, distance), pair)
        elif piece == PIECES - 1:
            whole = cols.at[slot]
            send(whole, whole, pair_sems, pair_at(kind, direction, distance), pair)

    def chunk_event(chunk):
        at = chunk_rows(chunk)
        arrived(peer_u.at[:, at], upd_sems, chunk)
        relay_u[:, at] = peer_u[:, at] + outgoing[:, at]
        if chunk == 0:
            arrived(relay_map.at[0, 0], map_sems, 1)
            send(relay_map.at[0, 0], places.at[2], map_sems, 2, across)
        send(relay_u.at[:, at], upper_u.at[:, at], upd_sems, CHUNKS + chunk, across)

    events = []

    def when(time, event, *operands):
        events.append((time, len(events), functools.partial(event, *operands)))

    hop = 2.0 + X_STEP
    for piece in range(PIECES):
        late = piece * X_STEP
        when(hop + late, row_event, 0, low_slot, piece, ((3, across), (4, y_pair)))
        when(hop + late, row_event, 1, across_slot, piece, ((5, y_pair),))
        when(2 * hop + late, row_event, 3, upper_slot, piece, ((6, y_pair),))
        when(Z_SHIFT + 3.0 + late, far_event, piece)
        for kind in range(2):
            for distance in range(1, half + 1):
                for direction in range(2):
                    if distance < half or piece == direction:
                        time = Z_SHIFT + Z_STEP * distance + 3.0 * kind + late
                        when(time, z_event, kind, direction, distance, piece)
    for chunk in range(CHUNKS):
        when(2.0 + X_STEP * (chunk + 1 + PIECES), chunk_event, chunk)
    for _, _, event in sorted(events, key=lambda entry: entry[:2]):
        event()

    for piece in range(PIECES):
        arrived(rows.at[y_slot, span(piece)], row_sems, row_at(2, piece))
    for message, bit in ((4, 2), (5, 6), (6, 4)):
        slot = flip(y_slot, 2) if bit != 4 else flip(y_slot, 4)
        slot = flip(slot, 4) if bit == 6 else slot
        for piece in range(PIECES):
            arrived(rows.at[slot, span(piece)], row_sems, row_at(message, piece))
    here[2].wait()
    here[3].wait()
    here[4].wait()

    depth = panel.shape[1]
    row_count = rows.shape[0] * part
    values = -rows[...].reshape(row_count, depth)
    high = values.astype(jnp.bfloat16)
    rest = (values - high.astype(jnp.float32)).astype(jnp.bfloat16)
    left[:, 0:depth] = high
    left[:, depth : 2 * depth] = high
    left[:, 2 * depth : 3 * depth] = rest

    def other(slot):
        return flip(slot, 1)

    arrived(cols.at[other(blk)], pair_sems, 0)
    arrived(cols.at[other(flip(blk, 2))], pair_sems, 1)
    for kind in range(2):
        for distance in range(1, half):
            for direction in range(2):
                slot = other(z_slot(kind, direction, distance))
                arrived(cols.at[slot], pair_sems, pair_at(kind, direction, distance))

    here_z = lax.div(blk, 4)
    group = 4 * part

    def multiply(z):
        right = cols[pl.ds(z * 4, 4)].reshape(group, depth)
        high = right.astype(jnp.bfloat16)
        rest = (right - high.astype(jnp.float32)).astype(jnp.bfloat16)
        right = jnp.concatenate([high, rest, high], axis=1)
        at = pl.ds(pl.multiple_of(z * group, group), group)
        product[:, at] = lax.dot_general(
            left[...],
            right,
            (((1,), (1,)), ((), ())),
            preferred_element_type=jnp.float32,
        )

    @pl.loop(0, z_count - 1)
    def _(step):
        multiply(lax.rem(here_z + half + 1 + step, z_count))

    for kind in range(2):
        for direction in range(2):
            slot = other(z_slot(kind, direction, half))
            at = pair_at(kind, direction, half)
            arrived(cols.at[slot, span(direction)], pair_sems, at)
    multiply(lax.rem(here_z + half, z_count))

    arrived(places.at[1], map_sems, 0)
    arrived(places.at[2], map_sems, 2)
    for chunk in range(CHUNKS):
        arrived(upper_u.at[:, chunk_rows(chunk)], upd_sems, CHUNKS + chunk)
    for copy in in_flight:
        copy.wait_send()


def place_kernel(
    product, own_u, peer_u, upper_u, places, out, front, sems
):
    slots, tile = own_u.shape[0], own_u.shape[1]
    tile_rows, tile_cols = front.shape[0] // tile, front.shape[1] // tile
    copies = []
    for tile_row in range(tile_rows):
        rows = pl.ds(tile_row * tile, tile)
        front[rows] = product[rows]

        def add(target, source, slot):
            @pl.when(lax.div(target, tile_cols) == tile_row)
            def _():
                col = lax.rem(target, tile_cols) * tile
                at = pl.ds(pl.multiple_of(col, tile), tile)
                front[rows, at] += source[slot]

        @pl.loop(0, slots)
        def _(slot):
            add(places[0, slot], own_u, slot)
            add(places[0, places[1, slot]], peer_u, slot)
            add(places[2, slot], upper_u, slot)

        copy = pltpu.make_async_copy(front.at[rows], out.at[rows], sems.at[tile_row])
        copy.start()
        copies.append(copy)
    for copy in copies:
        copy.wait()


def in_hbm(array):
    return pltpu.with_memory_space_constraint(array, pltpu.HBM)


def local(updates, pivot_panel, map_low, map_own, map_out):
    slots, tile = updates.shape[2], updates.shape[3]
    part, depth = pivot_panel.shape
    cubes, blks = lax.axis_size("cube"), lax.axis_size("blk")
    row_count, col_count = cubes * part, blks * part
    z_count = blks // 4
    half = z_count // 2
    f32, i32, bf16 = jnp.float32, jnp.int32, jnp.bfloat16
    dma = pltpu.SemaphoreType.DMA
    hbm = pl.BlockSpec(memory_space=pltpu.HBM)
    vmem = pl.BlockSpec(memory_space=pltpu.VMEM)
    smem = pl.BlockSpec(memory_space=pltpu.SMEM)
    z_messages = 2 + 4 * ((half - 1) * PIECES + 1)
    pair_messages = 2 + 4 * half
    blocks = pltpu.VMEM((slots, tile, tile), f32)
    own_u, peer_u, upper_u, product, places = pl.pallas_call(
        exchange_kernel,
        out_shape=(
            blocks,
            blocks,
            blocks,
            pltpu.VMEM((row_count, col_count), f32),
            pltpu.VMEM((3, slots), i32),
        ),
        in_specs=[hbm] * 5,
        out_specs=(vmem,) * 5,
        scratch_shapes=[
            pltpu.VMEM((cubes, part, depth), f32),
            pltpu.VMEM((blks, part, depth), f32),
            pltpu.VMEM((row_count, 3 * depth), bf16),
            pltpu.VMEM((slots, tile, tile), f32),
            pltpu.VMEM((slots, tile, tile), f32),
            pltpu.VMEM((1, 1, slots), i32),
            pltpu.SMEM((slots,), i32),
            dma((5,)),
            dma((7 * PIECES,)),
            dma((7 * PIECES,)),
            dma((z_messages,)),
            dma((z_messages,)),
            dma((pair_messages,)),
            dma((pair_messages,)),
            dma((2 * CHUNKS,)),
            dma((2 * CHUNKS,)),
            dma((3,)),
            dma((3,)),
        ],
        compiler_params=pltpu.CompilerParams(
            collective_id=0, has_side_effects=True, vmem_limit_bytes=24 << 20
        ),
    )(*(in_hbm(array) for array in (updates, pivot_panel, map_low, map_own, map_out)))
    out = pl.pallas_call(
        place_kernel,
        out_shape=jax.ShapeDtypeStruct((row_count, col_count), f32),
        in_specs=[vmem] * 4 + [smem],
        out_specs=hbm,
        scratch_shapes=[pltpu.VMEM((row_count, col_count), f32), dma((row_count // tile,))],
        compiler_params=pltpu.CompilerParams(vmem_limit_bytes=16 << 20),
    )(product, own_u, peer_u, upper_u, places)
    return out.reshape(cubes, 1, part, col_count)


def solution(mesh):
    placed = (
        P("cube", "blk", None, None, None),
        P(("cube", "blk"), None),
        P("cube", "blk", None),
        P("cube", "blk", None),
        P("cube", "blk", None),
    )
    return jax.shard_map(
        local, mesh=mesh, in_specs=placed, out_specs=P(None, "blk", None, "cube"), check_vma=False
    )
```

```python
import functools

import jax
import jax.numpy as jnp
from jax import lax
from jax.experimental import pallas as pl
from jax.experimental.pallas import tpu as pltpu
from jax.sharding import PartitionSpec as P

MESH = pl.DeviceIdType.MESH
CHUNKS = 8
PIECES = 2
FAR = 3
X_STEP = 0.55
Z_SHIFT = 0.0
Z_STEP = 2.3
B_OFF = 3.0
X_OFF = 2.0


def flip(index, bit):
    return index + bit - 2 * bit * lax.rem(lax.div(index, bit), 2)


def exchange_kernel(
    updates,
    panel,
    map_low,
    map_own,
    map_out,
    own_u,
    peer_u,
    upper_u,
    product,
    places,
    rows,
    cols,
    left,
    outgoing,
    relay_u,
    relay_map,
    low_scalars,
    local_sem,
    row_send,
    row_recv,
    col_send,
    col_recv,
    pair_send,
    pair_recv,
    upd_send,
    upd_recv,
    map_send,
    map_recv,
):
    cube, blk = lax.axis_index("cube"), lax.axis_index("blk")
    z_count = lax.axis_size("blk") // 4
    blk_count = 4 * z_count
    slots, tile = own_u.shape[0], own_u.shape[1]
    part = panel.shape[0]

    low = {"cube": flip(cube, 2), "blk": blk}
    across = {"cube": flip(flip(cube, 2), 4), "blk": blk}
    y_pair = {"cube": flip(cube, 1), "blk": blk}
    y_far = {"cube": cube, "blk": flip(blk, 2)}
    z_up = {"cube": cube, "blk": lax.rem(blk + 4, blk_count)}
    z_down = {"cube": cube, "blk": lax.rem(blk + blk_count - 4, blk_count)}
    pair = {"cube": cube, "blk": flip(blk, 1)}

    in_flight = []

    def send(src, dst, sems, at, device):
        copy = pltpu.make_async_remote_copy(
            src_ref=src,
            dst_ref=dst,
            send_sem=sems[0].at[at],
            recv_sem=sems[1].at[at],
            device_id=device,
            device_id_type=MESH,
        )
        copy.start()
        in_flight.append(copy)

    def arrived(dst, sems, at):
        pltpu.make_async_remote_copy(
            src_ref=dst,
            dst_ref=dst,
            send_sem=sems[0].at[at],
            recv_sem=sems[1].at[at],
            device_id=low,
            device_id_type=MESH,
        ).wait_recv()

    row_sems, col_sems = (row_send, row_recv), (col_send, col_recv)
    pair_sems, upd_sems = (pair_send, pair_recv), (upd_send, upd_recv)
    map_sems = (map_send, map_recv)

    def span(piece):
        return pl.ds(piece * (part // PIECES), part // PIECES)

    barrier = pltpu.get_barrier_semaphore()
    everyone = (low, across, y_pair, y_far, z_up, z_down, pair)
    for device in everyone:
        pl.semaphore_signal(barrier, inc=1, device_id=device, device_id_type=MESH)

    here = [
        pltpu.make_async_copy(map_low.at[0, 0], low_scalars, local_sem.at[0]),
        pltpu.make_async_copy(updates.at[0, 0], own_u, local_sem.at[1]),
        pltpu.make_async_copy(panel, rows.at[cube], local_sem.at[2]),
        pltpu.make_async_copy(panel, cols.at[blk], local_sem.at[3]),
        pltpu.make_async_copy(map_own.at[0, 0], places.at[0], local_sem.at[4]),
    ]
    for copy in here:
        copy.start()
    pl.semaphore_wait(barrier, len(everyone))

    def row_at(message, piece):
        return message * PIECES + piece

    def chunk_rows(chunk):
        return pl.ds(chunk * (tile // CHUNKS), tile // CHUNKS)

    for piece in range(PIECES):
        mine = panel.at[span(piece)]
        there = rows.at[cube, span(piece)]
        send(mine, there, row_sems, row_at(0, piece), low)
        send(mine, there, row_sems, row_at(1, piece), across)
        send(mine, there, row_sems, row_at(2, piece), y_pair)

    half = z_count // 2
    per_direction = (half - 1) * PIECES + 1

    def z_at(kind, direction, distance, piece):
        step = (distance - 1) * PIECES + (piece if distance < half else 0)
        return 2 + (kind * 2 + direction) * per_direction + step

    def z_slot(kind, direction, distance):
        shift = 4 * distance
        base = blk if kind == 0 else flip(blk, 2)
        return lax.rem(base + (blk_count - shift if direction == 0 else shift), blk_count)

    z_devices = (z_up, z_down)
    for piece in range(PIECES):
        for direction in range(2):
            send(
                panel.at[span(piece)],
                cols.at[blk, span(piece)],
                col_sems,
                z_at(0, direction, 1, piece),
                z_devices[direction],
            )
    for piece in range(PIECES):
        send(panel.at[span(piece)], cols.at[blk, span(piece)], col_sems, piece, y_far)
    send(panel, cols.at[blk], pair_sems, 0, pair)
    send(map_low.at[0, 0], places.at[1], map_sems, 0, low)
    send(map_out.at[0, 0], relay_map.at[0, 0], map_sems, 1, low)
    for chunk in range(CHUNKS):
        send(
            updates.at[0, 0, :, chunk_rows(chunk)],
            peer_u.at[:, chunk_rows(chunk)],
            upd_sems,
            chunk,
            low,
        )

    here[0].wait()
    here[1].wait()
    targets = [low_scalars[slot] for slot in range(slots)]

    @pl.loop(0, tile // 8)
    def _(step):
        at = pl.ds(pl.multiple_of(step * 8, 8), 8)
        blocks = [own_u[slot, at] for slot in range(slots)]
        for target in range(slots):
            terms = [
                blocks[slot] * jnp.where(targets[slot] == target, 1.0, 0.0)
                for slot in range(slots)
            ]
            while len(terms) > 1:
                terms = [a + b for a, b in zip(terms[::2], terms[1::2])]
            outgoing[target, at] = terms[0]

    low_slot = flip(cube, 2)
    across_slot = flip(flip(cube, 2), 4)
    upper_slot = flip(cube, 4)
    y_slot = flip(cube, 1)

    def row_event(message, slot, piece, forwards):
        there = rows.at[slot, span(piece)]
        arrived(there, row_sems, row_at(message, piece))
        for next_message, device in forwards:
            send(there, there, row_sems, row_at(next_message, piece), device)

    def far_event(piece):
        there = cols.at[flip(blk, 2), span(piece)]
        arrived(there, col_sems, piece)
        for direction in range(2):
            send(there, there, col_sems, z_at(1, direction, 1, piece), z_devices[direction])
        if piece == PIECES - 1:
            whole = cols.at[flip(blk, 2)]
            send(whole, whole, pair_sems, 1, pair)

    def pair_at(kind, direction, distance):
        return 2 + (kind * 2 + direction) * half + distance - 1

    def z_event(kind, direction, distance, piece):
        slot = z_slot(kind, direction, distance)
        there = cols.at[slot, span(piece)]
        arrived(there, col_sems, z_at(kind, direction, distance, piece))
        last = distance == half
        onward = distance + 1 < half or (distance + 1 == half and piece == direction)
        if kind == 1 and distance + 1 >= FAR:
            onward = False
        if kind == 0 and distance >= FAR:
            send(there, there, col_sems, z_at(1, direction, distance, piece), y_far)
        if onward:
            at = z_at(kind, direction, distance + 1, piece)
            send(there, there, col_sems, at, z_devices[direction])
        if last:
            send(there, there, pair_sems, pair_at(kind, direction, distance), pair)
        elif piece == PIECES - 1:
            whole = cols.at[slot]
            send(whole, whole, pair_sems, pair_at(kind, direction, distance), pair)

    def chunk_event(chunk):
        at = chunk_rows(chunk)
        arrived(peer_u.at[:, at], upd_sems, chunk)
        relay_u[:, at] = peer_u[:, at] + outgoing[:, at]
        if chunk == 0:
            arrived(relay_map.at[0, 0], map_sems, 1)
            send(relay_map.at[0, 0], places.at[2], map_sems, 2, across)
        send(relay_u.at[:, at], upper_u.at[:, at], upd_sems, CHUNKS + chunk, across)

    events = []

    def when(time, event, *operands):
        events.append((time, len(events), functools.partial(event, *operands)))

    hop = 2.0 + X_STEP
    for piece in range(PIECES):
        late = piece * X_STEP * 2 / PIECES
        when(hop + late, row_event, 0, low_slot, piece, ((3, across), (4, y_pair)))
        when(hop + late, row_event, 1, across_slot, piece, ((5, y_pair),))
        when(2 * hop + late, row_event, 3, upper_slot, piece, ((6, y_pair),))
        when(Z_SHIFT + B_OFF + late, far_event, piece)
        for kind in range(2):
            for distance in range(1, half + 1):
                for direction in range(2):
                    if distance < half or piece == direction:
                        time = Z_SHIFT + Z_STEP * distance + B_OFF * kind + late
                        when(time, z_event, kind, direction, distance, piece)
    for chunk in range(CHUNKS):
        when(X_OFF + X_STEP * (PIECES + (chunk + 1) * 16 / CHUNKS), chunk_event, chunk)
    for _, _, event in sorted(events, key=lambda entry: entry[:2]):
        event()

    for piece in range(PIECES):
        arrived(rows.at[y_slot, span(piece)], row_sems, row_at(2, piece))
    for message, bit in ((4, 2), (5, 6), (6, 4)):
        slot = flip(y_slot, 2) if bit != 4 else flip(y_slot, 4)
        slot = flip(slot, 4) if bit == 6 else slot
        for piece in range(PIECES):
            arrived(rows.at[slot, span(piece)], row_sems, row_at(message, piece))
    here[2].wait()
    here[3].wait()
    here[4].wait()

    depth = panel.shape[1]
    row_count = rows.shape[0] * part
    values = -rows[...].reshape(row_count, depth)
    high = values.astype(jnp.bfloat16)
    rest = (values - high.astype(jnp.float32)).astype(jnp.bfloat16)
    left[:, 0:depth] = high
    left[:, depth : 2 * depth] = high
    left[:, 2 * depth : 3 * depth] = rest

    def other(slot):
        return flip(slot, 1)

    here_z = lax.div(blk, 4)
    group = 4 * part

    def multiply(z):
        right = cols[pl.ds(z * 4, 4)].reshape(group, depth)
        high = right.astype(jnp.bfloat16)
        rest = (right - high.astype(jnp.float32)).astype(jnp.bfloat16)
        right = jnp.concatenate([high, rest, high], axis=1)
        at = pl.ds(pl.multiple_of(z * group, group), group)
        product[:, at] = lax.dot_general(
            left[...],
            right,
            (((1,), (1,)), ((), ())),
            preferred_element_type=jnp.float32,
        )

    def pairs_arrived(distance):
        for kind in range(2):
            for direction in range(2):
                slot = other(z_slot(kind, direction, distance))
                arrived(cols.at[slot], pair_sems, pair_at(kind, direction, distance))

    arrived(cols.at[other(blk)], pair_sems, 0)
    arrived(cols.at[other(flip(blk, 2))], pair_sems, 1)
    for distance in range(1, half - 1):
        pairs_arrived(distance)

    @pl.loop(0, z_count - 3)
    def _(step):
        multiply(lax.rem(here_z + half + 2 + step, z_count))

    pairs_arrived(half - 1)
    for shift in (half + 1, half - 1):
        multiply(lax.rem(here_z + shift, z_count))

    for kind in range(2):
        for direction in range(2):
            slot = other(z_slot(kind, direction, half))
            at = pair_at(kind, direction, half)
            arrived(cols.at[slot, span(direction)], pair_sems, at)
    multiply(lax.rem(here_z + half, z_count))

    arrived(places.at[1], map_sems, 0)
    arrived(places.at[2], map_sems, 2)
    for chunk in range(CHUNKS):
        arrived(upper_u.at[:, chunk_rows(chunk)], upd_sems, CHUNKS + chunk)
    for copy in in_flight:
        copy.wait_send()


def place_kernel(product, own_u, peer_u, upper_u, places, front, out, sems):
    slots, tile = own_u.shape[0], own_u.shape[1]
    tile_rows, tile_cols = front.shape[0] // tile, front.shape[1] // tile

    def add(target, blocks, slot):
        row = pl.multiple_of(lax.div(target, tile_cols) * tile, tile)
        col = pl.multiple_of(lax.rem(target, tile_cols) * tile, tile)
        front[pl.ds(row, tile), pl.ds(col, tile)] += blocks[slot]

    @pl.loop(0, slots)
    def _(slot):
        add(places[0, slot], own_u, slot)
        add(places[0, places[1, slot]], peer_u, slot)
        add(places[2, slot], upper_u, slot)

    copies = []
    for tile_row in range(tile_rows):
        rows = pl.ds(tile_row * tile, tile)
        copy = pltpu.make_async_copy(front.at[rows], out.at[rows], sems.at[tile_row])
        copy.start()
        copies.append(copy)
    for copy in copies:
        copy.wait()


def in_hbm(array):
    return pltpu.with_memory_space_constraint(array, pltpu.HBM)


def local(updates, pivot_panel, map_low, map_own, map_out):
    slots, tile = updates.shape[2], updates.shape[3]
    part, depth = pivot_panel.shape
    cubes, blks = lax.axis_size("cube"), lax.axis_size("blk")
    row_count, col_count = cubes * part, blks * part
    z_count = blks // 4
    half = z_count // 2
    f32, i32, bf16 = jnp.float32, jnp.int32, jnp.bfloat16
    dma = pltpu.SemaphoreType.DMA
    hbm = pl.BlockSpec(memory_space=pltpu.HBM)
    vmem = pl.BlockSpec(memory_space=pltpu.VMEM)
    smem = pl.BlockSpec(memory_space=pltpu.SMEM)
    z_messages = 2 + 4 * ((half - 1) * PIECES + 1)
    pair_messages = 2 + 4 * half
    blocks = pltpu.VMEM((slots, tile, tile), f32)
    own_u, peer_u, upper_u, product, places = pl.pallas_call(
        exchange_kernel,
        out_shape=(
            blocks,
            blocks,
            blocks,
            pltpu.VMEM((row_count, col_count), f32),
            pltpu.VMEM((3, slots), i32),
        ),
        in_specs=[hbm] * 5,
        out_specs=(vmem,) * 5,
        scratch_shapes=[
            pltpu.VMEM((cubes, part, depth), f32),
            pltpu.VMEM((blks, part, depth), f32),
            pltpu.VMEM((row_count, 3 * depth), bf16),
            pltpu.VMEM((slots, tile, tile), f32),
            pltpu.VMEM((slots, tile, tile), f32),
            pltpu.VMEM((1, 1, slots), i32),
            pltpu.SMEM((slots,), i32),
            dma((5,)),
            dma((7 * PIECES,)),
            dma((7 * PIECES,)),
            dma((z_messages,)),
            dma((z_messages,)),
            dma((pair_messages,)),
            dma((pair_messages,)),
            dma((2 * CHUNKS,)),
            dma((2 * CHUNKS,)),
            dma((3,)),
            dma((3,)),
        ],
        compiler_params=pltpu.CompilerParams(
            collective_id=0, has_side_effects=True, vmem_limit_bytes=24 << 20
        ),
    )(*(in_hbm(array) for array in (updates, pivot_panel, map_low, map_own, map_out)))
    _, out = pl.pallas_call(
        place_kernel,
        out_shape=(
            pltpu.VMEM((row_count, col_count), f32),
            jax.ShapeDtypeStruct((row_count, col_count), f32),
        ),
        in_specs=[vmem] * 4 + [smem],
        out_specs=(vmem, hbm),
        scratch_shapes=[dma((row_count // tile,))],
        input_output_aliases={0: 0},
        compiler_params=pltpu.CompilerParams(vmem_limit_bytes=16 << 20),
    )(product, own_u, peer_u, upper_u, places)
    return out.reshape(cubes, 1, part, col_count)


def solution(mesh):
    placed = (
        P("cube", "blk", None, None, None),
        P(("cube", "blk"), None),
        P("cube", "blk", None),
        P("cube", "blk", None),
        P("cube", "blk", None),
    )
    return jax.shard_map(
        local, mesh=mesh, in_specs=placed, out_specs=P(None, "blk", None, "cube"), check_vma=False
    )
```

```python
import functools

import jax
import jax.numpy as jnp
from jax import lax
from jax.experimental import pallas as pl
from jax.experimental.pallas import tpu as pltpu
from jax.sharding import PartitionSpec as P

MESH = pl.DeviceIdType.MESH
CHUNKS = 8
PIECES = 2
FAR = 3
X_STEP = 0.55
Z_SHIFT = 0.0
Z_STEP = 2.3
B_OFF = 3.0
X_OFF = 2.5


def flip(index, bit):
    return index + bit - 2 * bit * lax.rem(lax.div(index, bit), 2)


def exchange_kernel(
    updates,
    panel,
    map_low,
    map_own,
    map_out,
    own_u,
    peer_u,
    upper_u,
    product,
    places,
    rows,
    cols,
    left,
    outgoing,
    relay_u,
    relay_map,
    low_scalars,
    local_sem,
    row_send,
    row_recv,
    col_send,
    col_recv,
    pair_send,
    pair_recv,
    upd_send,
    upd_recv,
    map_send,
    map_recv,
):
    cube, blk = lax.axis_index("cube"), lax.axis_index("blk")
    z_count = lax.axis_size("blk") // 4
    blk_count = 4 * z_count
    slots, tile = own_u.shape[0], own_u.shape[1]
    part = panel.shape[0]

    low = {"cube": flip(cube, 2), "blk": blk}
    across = {"cube": flip(flip(cube, 2), 4), "blk": blk}
    y_pair = {"cube": flip(cube, 1), "blk": blk}
    y_far = {"cube": cube, "blk": flip(blk, 2)}
    z_up = {"cube": cube, "blk": lax.rem(blk + 4, blk_count)}
    z_down = {"cube": cube, "blk": lax.rem(blk + blk_count - 4, blk_count)}
    pair = {"cube": cube, "blk": flip(blk, 1)}

    in_flight = []

    def send(src, dst, sems, at, device):
        copy = pltpu.make_async_remote_copy(
            src_ref=src,
            dst_ref=dst,
            send_sem=sems[0].at[at],
            recv_sem=sems[1].at[at],
            device_id=device,
            device_id_type=MESH,
        )
        copy.start()
        in_flight.append(copy)

    def arrived(dst, sems, at):
        pltpu.make_async_remote_copy(
            src_ref=dst,
            dst_ref=dst,
            send_sem=sems[0].at[at],
            recv_sem=sems[1].at[at],
            device_id=low,
            device_id_type=MESH,
        ).wait_recv()

    row_sems, col_sems = (row_send, row_recv), (col_send, col_recv)
    pair_sems, upd_sems = (pair_send, pair_recv), (upd_send, upd_recv)
    map_sems = (map_send, map_recv)

    def span(piece):
        return pl.ds(piece * (part // PIECES), part // PIECES)

    barrier = pltpu.get_barrier_semaphore()
    everyone = (low, across, y_pair, y_far, z_up, z_down, pair)
    for device in everyone:
        pl.semaphore_signal(barrier, inc=1, device_id=device, device_id_type=MESH)

    here = [
        pltpu.make_async_copy(map_low.at[0, 0], low_scalars, local_sem.at[0]),
        pltpu.make_async_copy(updates.at[0, 0], own_u, local_sem.at[1]),
        pltpu.make_async_copy(panel, rows.at[cube], local_sem.at[2]),
        pltpu.make_async_copy(panel, cols.at[blk], local_sem.at[3]),
        pltpu.make_async_copy(map_own.at[0, 0], places.at[0], local_sem.at[4]),
    ]
    for copy in here:
        copy.start()
    pl.semaphore_wait(barrier, len(everyone))

    def row_at(message, piece):
        return message * PIECES + piece

    def chunk_rows(chunk):
        return pl.ds(chunk * (tile // CHUNKS), tile // CHUNKS)

    for piece in range(PIECES):
        send(panel.at[span(piece)], cols.at[blk, span(piece)], col_sems, piece, y_far)
    half = z_count // 2
    per_direction = (half - 1) * PIECES + 1

    def z_at(kind, direction, distance, piece):
        step = (distance - 1) * PIECES + (piece if distance < half else 0)
        return 2 + (kind * 2 + direction) * per_direction + step

    def z_slot(kind, direction, distance):
        shift = 4 * distance
        base = blk if kind == 0 else flip(blk, 2)
        return lax.rem(base + (blk_count - shift if direction == 0 else shift), blk_count)

    z_devices = (z_up, z_down)
    for piece in range(PIECES):
        for direction in range(2):
            send(
                panel.at[span(piece)],
                cols.at[blk, span(piece)],
                col_sems,
                z_at(0, direction, 1, piece),
                z_devices[direction],
            )
    for piece in range(PIECES):
        mine = panel.at[span(piece)]
        there = rows.at[cube, span(piece)]
        send(mine, there, row_sems, row_at(0, piece), low)
        send(mine, there, row_sems, row_at(1, piece), across)
        send(mine, there, row_sems, row_at(2, piece), y_pair)
    send(panel, cols.at[blk], pair_sems, 0, pair)
    send(map_low.at[0, 0], places.at[1], map_sems, 0, low)
    send(map_out.at[0, 0], relay_map.at[0, 0], map_sems, 1, low)
    for chunk in range(CHUNKS):
        send(
            updates.at[0, 0, :, chunk_rows(chunk)],
            peer_u.at[:, chunk_rows(chunk)],
            upd_sems,
            chunk,
            low,
        )

    here[0].wait()
    here[1].wait()
    targets = [low_scalars[slot] for slot in range(slots)]

    @pl.loop(0, tile // 8)
    def _(step):
        at = pl.ds(pl.multiple_of(step * 8, 8), 8)
        blocks = [own_u[slot, at] for slot in range(slots)]
        for target in range(slots):
            terms = [
                blocks[slot] * jnp.where(targets[slot] == target, 1.0, 0.0)
                for slot in range(slots)
            ]
            while len(terms) > 1:
                terms = [a + b for a, b in zip(terms[::2], terms[1::2])]
            outgoing[target, at] = terms[0]

    low_slot = flip(cube, 2)
    across_slot = flip(flip(cube, 2), 4)
    upper_slot = flip(cube, 4)
    y_slot = flip(cube, 1)

    def row_event(message, slot, piece, forwards):
        there = rows.at[slot, span(piece)]
        arrived(there, row_sems, row_at(message, piece))
        for next_message, device in forwards:
            send(there, there, row_sems, row_at(next_message, piece), device)

    def far_event(piece):
        there = cols.at[flip(blk, 2), span(piece)]
        arrived(there, col_sems, piece)
        for direction in range(2):
            send(there, there, col_sems, z_at(1, direction, 1, piece), z_devices[direction])
        if piece == PIECES - 1:
            whole = cols.at[flip(blk, 2)]
            send(whole, whole, pair_sems, 1, pair)

    def pair_at(kind, direction, distance):
        return 2 + (kind * 2 + direction) * half + distance - 1

    def z_event(kind, direction, distance, piece):
        slot = z_slot(kind, direction, distance)
        there = cols.at[slot, span(piece)]
        arrived(there, col_sems, z_at(kind, direction, distance, piece))
        last = distance == half
        onward = distance + 1 < half or (distance + 1 == half and piece == direction)
        if kind == 1 and distance + 1 >= (3, 2)[direction]:
            onward = False
        if kind == 0 and distance >= (3, 2)[direction]:
            send(there, there, col_sems, z_at(1, direction, distance, piece), y_far)
        if onward:
            at = z_at(kind, direction, distance + 1, piece)
            send(there, there, col_sems, at, z_devices[direction])
        if last:
            send(there, there, pair_sems, pair_at(kind, direction, distance), pair)
        elif piece == PIECES - 1:
            whole = cols.at[slot]
            send(whole, whole, pair_sems, pair_at(kind, direction, distance), pair)

    def chunk_event(chunk):
        at = chunk_rows(chunk)
        arrived(peer_u.at[:, at], upd_sems, chunk)
        relay_u[:, at] = peer_u[:, at] + outgoing[:, at]
        if chunk == 0:
            arrived(relay_map.at[0, 0], map_sems, 1)
            send(relay_map.at[0, 0], places.at[2], map_sems, 2, across)
        send(relay_u.at[:, at], upper_u.at[:, at], upd_sems, CHUNKS + chunk, across)

    events = []

    def when(time, event, *operands):
        events.append((time, len(events), functools.partial(event, *operands)))

    hop = 2.0 + X_STEP
    for piece in range(PIECES):
        late = piece * X_STEP * 2 / PIECES
        when(hop + late, row_event, 0, low_slot, piece, ((3, across), (4, y_pair)))
        when(hop + late, row_event, 1, across_slot, piece, ((5, y_pair),))
        when(2 * hop + late, row_event, 3, upper_slot, piece, ((6, y_pair),))
        when(Z_SHIFT + B_OFF + late, far_event, piece)
        for kind in range(2):
            for distance in range(1, half + 1):
                for direction in range(2):
                    if distance < half or piece == direction:
                        time = Z_SHIFT + Z_STEP * distance + B_OFF * kind + late
                        when(time, z_event, kind, direction, distance, piece)
    for chunk in range(CHUNKS):
        when(X_OFF + X_STEP * (PIECES + (chunk + 1) * 16 / CHUNKS), chunk_event, chunk)
    for _, _, event in sorted(events, key=lambda entry: entry[:2]):
        event()

    for piece in range(PIECES):
        arrived(rows.at[y_slot, span(piece)], row_sems, row_at(2, piece))
    for message, bit in ((4, 2), (5, 6), (6, 4)):
        slot = flip(y_slot, 2) if bit != 4 else flip(y_slot, 4)
        slot = flip(slot, 4) if bit == 6 else slot
        for piece in range(PIECES):
            arrived(rows.at[slot, span(piece)], row_sems, row_at(message, piece))
    here[2].wait()
    here[3].wait()
    here[4].wait()

    depth = panel.shape[1]
    row_count = rows.shape[0] * part
    values = -rows[...].reshape(row_count, depth)
    high = values.astype(jnp.bfloat16)
    rest = (values - high.astype(jnp.float32)).astype(jnp.bfloat16)
    left[:, 0:depth] = high
    left[:, depth : 2 * depth] = high
    left[:, 2 * depth : 3 * depth] = rest

    def other(slot):
        return flip(slot, 1)

    here_z = lax.div(blk, 4)
    group = 4 * part

    def multiply(z):
        right = cols[pl.ds(z * 4, 4)].reshape(group, depth)
        high = right.astype(jnp.bfloat16)
        rest = (right - high.astype(jnp.float32)).astype(jnp.bfloat16)
        right = jnp.concatenate([high, rest, high], axis=1)
        at = pl.ds(pl.multiple_of(z * group, group), group)
        product[:, at] = lax.dot_general(
            left[...],
            right,
            (((1,), (1,)), ((), ())),
            preferred_element_type=jnp.float32,
        )

    def pairs_arrived(distance):
        for kind in range(2):
            for direction in range(2):
                slot = other(z_slot(kind, direction, distance))
                arrived(cols.at[slot], pair_sems, pair_at(kind, direction, distance))

    arrived(cols.at[other(blk)], pair_sems, 0)
    arrived(cols.at[other(flip(blk, 2))], pair_sems, 1)
    for distance in range(1, half - 1):
        pairs_arrived(distance)

    @pl.loop(0, z_count - 3)
    def _(step):
        multiply(lax.rem(here_z + half + 2 + step, z_count))

    pairs_arrived(half - 1)
    for shift in (half + 1, half - 1):
        multiply(lax.rem(here_z + shift, z_count))

    for kind in range(2):
        for direction in range(2):
            slot = other(z_slot(kind, direction, half))
            at = pair_at(kind, direction, half)
            arrived(cols.at[slot, span(direction)], pair_sems, at)
    multiply(lax.rem(here_z + half, z_count))

    arrived(places.at[1], map_sems, 0)
    arrived(places.at[2], map_sems, 2)
    for chunk in range(CHUNKS):
        arrived(upper_u.at[:, chunk_rows(chunk)], upd_sems, CHUNKS + chunk)
    for copy in in_flight:
        copy.wait_send()


def place_kernel(product, own_u, peer_u, upper_u, places, front, out, sems):
    slots, tile = own_u.shape[0], own_u.shape[1]
    tile_rows, tile_cols = front.shape[0] // tile, front.shape[1] // tile

    def add(target, blocks, slot):
        row = pl.multiple_of(lax.div(target, tile_cols) * tile, tile)
        col = pl.multiple_of(lax.rem(target, tile_cols) * tile, tile)
        front[pl.ds(row, tile), pl.ds(col, tile)] += blocks[slot]

    for slot in range(slots):
        add(places[0, slot], own_u, slot)
        add(places[0, places[1, slot]], peer_u, slot)
        add(places[2, slot], upper_u, slot)

    copies = []
    for tile_row in range(tile_rows):
        rows = pl.ds(tile_row * tile, tile)
        copy = pltpu.make_async_copy(front.at[rows], out.at[rows], sems.at[tile_row])
        copy.start()
        copies.append(copy)
    for copy in copies:
        copy.wait()


def in_hbm(array):
    return pltpu.with_memory_space_constraint(array, pltpu.HBM)


def local(updates, pivot_panel, map_low, map_own, map_out):
    slots, tile = updates.shape[2], updates.shape[3]
    part, depth = pivot_panel.shape
    cubes, blks = lax.axis_size("cube"), lax.axis_size("blk")
    row_count, col_count = cubes * part, blks * part
    z_count = blks // 4
    half = z_count // 2
    f32, i32, bf16 = jnp.float32, jnp.int32, jnp.bfloat16
    dma = pltpu.SemaphoreType.DMA
    hbm = pl.BlockSpec(memory_space=pltpu.HBM)
    vmem = pl.BlockSpec(memory_space=pltpu.VMEM)
    smem = pl.BlockSpec(memory_space=pltpu.SMEM)
    z_messages = 2 + 4 * ((half - 1) * PIECES + 1)
    pair_messages = 2 + 4 * half
    blocks = pltpu.VMEM((slots, tile, tile), f32)
    own_u, peer_u, upper_u, product, places = pl.pallas_call(
        exchange_kernel,
        out_shape=(
            blocks,
            blocks,
            blocks,
            pltpu.VMEM((row_count, col_count), f32),
            pltpu.VMEM((3, slots), i32),
        ),
        in_specs=[hbm] * 5,
        out_specs=(vmem,) * 5,
        scratch_shapes=[
            pltpu.VMEM((cubes, part, depth), f32),
            pltpu.VMEM((blks, part, depth), f32),
            pltpu.VMEM((row_count, 3 * depth), bf16),
            pltpu.VMEM((slots, tile, tile), f32),
            pltpu.VMEM((slots, tile, tile), f32),
            pltpu.VMEM((1, 1, slots), i32),
            pltpu.SMEM((slots,), i32),
            dma((5,)),
            dma((7 * PIECES,)),
            dma((7 * PIECES,)),
            dma((z_messages,)),
            dma((z_messages,)),
            dma((pair_messages,)),
            dma((pair_messages,)),
            dma((2 * CHUNKS,)),
            dma((2 * CHUNKS,)),
            dma((3,)),
            dma((3,)),
        ],
        compiler_params=pltpu.CompilerParams(
            collective_id=0, has_side_effects=True, vmem_limit_bytes=24 << 20
        ),
    )(*(in_hbm(array) for array in (updates, pivot_panel, map_low, map_own, map_out)))
    _, out = pl.pallas_call(
        place_kernel,
        out_shape=(
            pltpu.VMEM((row_count, col_count), f32),
            jax.ShapeDtypeStruct((row_count, col_count), f32),
        ),
        in_specs=[vmem] * 4 + [smem],
        out_specs=(vmem, hbm),
        scratch_shapes=[dma((row_count // tile,))],
        input_output_aliases={0: 0},
        compiler_params=pltpu.CompilerParams(vmem_limit_bytes=16 << 20),
    )(product, own_u, peer_u, upper_u, places)
    return out.reshape(cubes, 1, part, col_count)


def solution(mesh):
    placed = (
        P("cube", "blk", None, None, None),
        P(("cube", "blk"), None),
        P("cube", "blk", None),
        P("cube", "blk", None),
        P("cube", "blk", None),
    )
    return jax.shard_map(
        local, mesh=mesh, in_specs=placed, out_specs=P(None, "blk", None, "cube"), check_vma=False
    )
```
